32 devices in a mesh: groups: 2 (over x), tower: 2 (over core), inner: 8 (over z, y).
Axes of the slice: x: 2, y: 2, z: 4, core: 2. Of those that a mesh axis runs over, the one named last changes fastest.
Arguments:
- ids: int32 [2, 64, 2048, 4], P('tower', 'inner', 'groups'), parts along dimension 2, may hold values from 0 to 16383
- bag_len: int32 [2, 64, 2048], P('tower', 'inner', 'groups'), parts along dimension 2, may hold values from 1 to 4
- slot_of_feature: int32 [2, 64], P('tower'), may hold values from 0 to 63, each once within a row
- tables: bfloat16 [2, 64, 16384, 24], P('tower', 'inner'), may hold values from -3 to 3
- cross_w: bfloat16 [2, 1536, 1536], P('tower'), may hold values from -0.15625 to 0.15625
- cross_b: float32 [2, 1536], P('tower'), may hold values from -3 to 3
- comp_w: bfloat16 [2, 1536, 64], P('tower'), may hold values from -0.15625 to 0.15625
- comp_b: float32 [2, 64], P('tower'), may hold values from -3 to 3
- other_towers: bfloat16 [2048, 896], P(('groups', 'inner')), parts along dimension 0, may hold values from -6 to 6
- expert_w: bfloat16 [8, 1024, 512], P('tower'), may hold values from -0.1875 to 0.1875
- expert_b: float32 [8, 512], P('tower'), may hold values from -3 to 3
- gate_w: bfloat16 [1024, 4, 8], replicated, may hold values from -0.1875 to 0.1875
Outputs:
- task_mix: bfloat16 [2048, 4, 512], P(('groups', 'inner'), None, 'tower'), parts along dimension 0
The draws below stay inside these ranges and needn't reach their ends.
There are 2 independent parts, one for each index of `groups`. The reference program is written for one: setup_inputs(seed, part) draws one part's arguments, and reference() takes and returns one part's arrays. A program takes and returns all parts, laid end to end along the dimension named above; an argument that names none is the same for every part. Nothing has to cross between parts.
Inputs may be any that keep to these rules, and one draw needn't show every extreme that they name: `bag_len`: every bag holds at least one id. `slot_of_feature`: each row is a permutation of the 64 slots.
All inputs are finite; a program needn't handle non-finite values.
Results may differ from the reference program's by a relative error of at most 0.0095.
Values may be sent and summed in bfloat16 or wider, within the bound.
A program may use at most 128 MiB of HBM per device.

```python
import math
import jax
import jax.numpy as jnp
import numpy as np
from jax import lax

WIDTH = 1536
NF = 64
ED = 24
VOCAB = 16384
BAG = 4
CW = 64
EIN = 1024
HID = 512
TASKS = 4
TOWERS = 2
EXPERTS = 8
OTHER = 896
SAMPLES = 1024


def with_ends(result, key, low, high):
    longest = result.shape.index(max(result.shape))
    spots = []
    for shift in (0, 1):
        where = [jax.random.randint(jax.random.fold_in(key, axis), (), 0, length) for axis, length in enumerate(result.shape)]
        where[longest] = (where[longest] + shift) % result.shape[longest]
        spots.append(tuple(where))
    return result.at[spots[0]].set(low).at[spots[1]].set(high)


def levels(rng, shape, pieces, least, high):
    factor_of, own = 1.0, jax.random.fold_in(rng, 6)
    for axis_at, blocks in pieces:
        draws = jnp.exp(jax.random.uniform(jax.random.fold_in(own, axis_at), (blocks,), jnp.float32, least / len(pieces), high / len(pieces)))
        factor_of = factor_of * jnp.repeat(draws, shape[axis_at] // blocks).reshape([-1 if axis == axis_at else 1 for axis in range(len(shape))])
    return factor_of


def cumulative_ranks(amount, slope):
    loads = [(1 << 20) // math.isqrt(standing ** slope) + 1 for standing in range(1, amount + 1)]
    scale = 1 + sum(loads) // (1 << 30)
    return np.cumsum(np.array([max(1, weight // scale) for weight in loads]))


def ranked(rng, shape, amount, lean):
    grid = cumulative_ranks(amount, lean)
    lot = jax.random.randint(jax.random.fold_in(rng, 1), shape, 0, int(grid[amount - 1]))
    standing = jnp.searchsorted(jnp.asarray(grid, jnp.int32), lot, side="right")
    return jax.random.permutation(jax.random.fold_in(rng, 2), amount)[standing].astype(jnp.int32)


def centred(own_key, dims, spread, bound, split=(), dtype=jnp.bfloat16):
    gain = levels(own_key, dims, split, -0.22, 0.18) if split else 1.0
    values = jax.random.normal(own_key, dims, jnp.float32) * spread * gain
    return jnp.minimum(jnp.maximum(values, -bound), bound).astype(dtype)


def setup_inputs(seed: int = 0, part: int = 0) -> dict:
    streams_of = jax.random.split(jax.random.key(seed), 13)
    part_splits = jax.random.split(jax.random.fold_in(streams_of[12], part), 13)
    ids = with_ends(ranked(part_splits[0], (TOWERS, NF, SAMPLES, BAG), VOCAB, 2), jax.random.fold_in(part_splits[0], 3), 0, VOCAB - 1).astype(jnp.int32)
    bag_len = with_ends(jax.random.randint(part_splits[1], (TOWERS, NF, SAMPLES), 1, BAG + 1), jax.random.fold_in(part_splits[1], 1), 1, BAG).astype(jnp.int32)
    slot_of_feature = jax.vmap(lambda own: jax.random.permutation(own, NF))(jax.random.split(streams_of[2], TOWERS)).reshape((TOWERS, NF)).astype(jnp.int32)
    tables = centred(streams_of[3], (TOWERS, NF, VOCAB, ED), 0.5, 3.0, ((0, 2), (1, 8)))
    cross_w = centred(streams_of[4], (TOWERS, WIDTH, WIDTH), WIDTH ** -0.5, 0.15625, ((0, 2),))
    cross_b = centred(streams_of[5], (TOWERS, WIDTH), 0.5, 3.0, ((0, 2),), jnp.float32)
    comp_w = centred(streams_of[6], (TOWERS, WIDTH, CW), WIDTH ** -0.5, 0.15625, ((0, 2),))
    comp_b = centred(streams_of[7], (TOWERS, CW), 0.5, 3.0, ((0, 2),), jnp.float32)
    other_towers = centred(part_splits[8], (SAMPLES, OTHER), 1.0, 6.0, ((0, 8),))
    expert_w = centred(streams_of[9], (EXPERTS, EIN, HID), EIN ** -0.5, 0.1875, ((0, 2),))
    expert_b = centred(streams_of[10], (EXPERTS, HID), 0.5, 3.0, ((0, 2),), jnp.float32)
    gate_w = centred(streams_of[11], (EIN, TASKS, EXPERTS), EIN ** -0.5, 0.1875)
    return {"ids": ids, "bag_len": bag_len, "slot_of_feature": slot_of_feature, "tables": tables, "cross_w": cross_w, "cross_b": cross_b, "comp_w": comp_w, "comp_b": comp_b, "other_towers": other_towers, "expert_w": expert_w, "expert_b": expert_b, "gate_w": gate_w}


def pool_feature(lookup, indices, lengths):
    gathered = jnp.take(lookup, indices, axis=0)
    in_bag = jnp.arange(indices.shape[1])[None, :] < lengths[:, None]
    summed = jnp.sum(jnp.where(in_bag[:, :, None], gathered.astype(jnp.float32), 0.0), axis=1)
    return summed.astype(jnp.bfloat16)


def reference(ids, bag_len, slot_of_feature, tables, cross_w, cross_b, comp_w, comp_b, other_towers, expert_w, expert_b, gate_w):
    flat_tables = tables.reshape(TOWERS * NF, VOCAB, ED)
    flat_ids = ids.reshape(TOWERS * NF, SAMPLES, BAG)
    flat_len = bag_len.reshape(TOWERS * NF, SAMPLES)
    pooled = lax.map(lambda packed: pool_feature(packed[0], packed[1], packed[2]), (flat_tables, flat_ids, flat_len))
    pooled = pooled.reshape(TOWERS, NF, SAMPLES, ED)
    outputs = []
    for tower in range(TOWERS):
        onehot = (slot_of_feature[tower][:, None] == jnp.arange(NF)[None, :]).astype(jnp.float32)
        first_layer = jnp.einsum('fsd,fg->sgd', pooled[tower].astype(jnp.float32), onehot).astype(jnp.bfloat16).reshape(SAMPLES, WIDTH)
        crossed = jnp.dot(first_layer, cross_w[tower], preferred_element_type=jnp.float32) + cross_b[tower]
        base = first_layer.astype(jnp.float32)
        next_layer = (base * crossed + base).astype(jnp.bfloat16)
        squeezed = jnp.dot(next_layer, comp_w[tower], preferred_element_type=jnp.float32) + comp_b[tower]
        outputs.append(squeezed.astype(jnp.bfloat16))
    expert_in = jnp.concatenate([other_towers] + outputs, axis=1)
    logits = jnp.einsum('ri,ike->rke', expert_in.astype(jnp.float32), gate_w.astype(jnp.float32))
    weights = jnp.exp(logits)
    gate_probs = weights / jnp.sum(weights, axis=2, keepdims=True)

    def add_expert(running, packed):
        matrix, bias, member = packed
        hidden = jnp.maximum(jnp.dot(expert_in, matrix, preferred_element_type=jnp.float32) + bias, 0.0).astype(jnp.bfloat16)
        chosen = jnp.sum(gate_probs * (jnp.arange(EXPERTS) == member).astype(jnp.float32)[None, None, :], axis=2)
        return running + chosen[:, :, None] * hidden.astype(jnp.float32)[:, None, :], None

    start = jnp.zeros((SAMPLES, TASKS, HID), jnp.float32)
    running, unused = lax.scan(add_expert, start, (expert_w, expert_b, jnp.arange(EXPERTS).astype(jnp.int32)))
    return running.astype(jnp.bfloat16)
```

```python
import functools
import jax
import jax.numpy as jnp
from jax import lax
from jax.experimental import pallas as pl
from jax.experimental.pallas import tpu as pltpu
from jax.sharding import PartitionSpec as P

MESH = pl.DeviceIdType.MESH


def pool_kernel(bag, unroll, ids_ref, tab_ref, out_ref, rows_ref, acc_ref):
    group, width, vocab = tab_ref.shape
    dests, _, block = out_ref.shape
    samples = dests * block
    lanes = rows_ref.shape[1]
    first = pl.program_id(0) * (group * bag * samples)

    def turn(c, carry):
        at = pl.multiple_of(c * lanes, lanes)
        parts = [tab_ref[f, :, pl.ds(at, lanes)].astype(jnp.float32) for f in range(group)]
        if lanes > group * width:
            parts.append(jnp.zeros((lanes - group * width, lanes), jnp.float32))
        rows_ref[pl.ds(at, lanes), :] = jnp.concatenate(parts, axis=0).T
        return carry

    lax.fori_loop(0, vocab // lanes, turn, 0)
    rows_ref[pl.ds(vocab, 8), :] = jnp.zeros((8, lanes), jnp.float32)
    lane = lax.broadcasted_iota(jnp.int32, (1, lanes), 1)
    inside = [lane < (f + 1) * width for f in range(group)]

    def look(n, carry):
        base = n * unroll
        for u in range(unroll):
            total = None
            for f in reversed(range(group)):
                got = [
                    rows_ref[pl.ds(ids_ref[first + (f * bag + j) * samples + base + u], 1), :]
                    for j in range(bag)
                ]
                while len(got) > 1:
                    got = [a + b for a, b in zip(got[::2], got[1::2])] + got[len(got) & ~1 :]
                total = got[0] if total is None else jnp.where(inside[f], got[0], total)
            acc_ref[pl.ds(base + u, 1), :] = total
        return carry

    lax.fori_loop(0, samples // unroll, look, 0)
    for d in range(dests):
        turned = acc_ref[pl.ds(d * block, block), :].T
        out_ref[d] = turned[: group * width].astype(out_ref.dtype)


def pool(tables, ids, lengths, dests, unroll=16):
    features, vocab, width = tables.shape
    samples, bag = ids.shape[1:]
    group = max(g for g in range(1, features + 1) if features % g == 0 and g * width <= 128)
    in_bag = jnp.arange(bag)[None, :, None] < lengths[:, None, :]
    flat = jnp.where(in_bag, jnp.transpose(ids, (0, 2, 1)), vocab).reshape(-1)
    return pl.pallas_call(
        functools.partial(pool_kernel, bag, unroll),
        out_shape=jax.ShapeDtypeStruct((dests, features * width, samples // dests), jnp.bfloat16),
        grid_spec=pltpu.PrefetchScalarGridSpec(
            num_scalar_prefetch=1,
            grid=(features // group,),
            in_specs=[pl.BlockSpec((group, width, vocab), lambda i, ids: (i, 0, 0))],
            out_specs=pl.BlockSpec((dests, group * width, samples // dests), lambda i, ids: (0, i, 0)),
            scratch_shapes=[
                pltpu.VMEM((vocab + 8, 128), jnp.float32),
                pltpu.VMEM((samples, 128), jnp.float32),
            ],
        ),
        compiler_params=pltpu.CompilerParams(vmem_limit_bytes=48 * 2**20),
    )(flat, jnp.transpose(tables, (0, 2, 1)))


def dense_kernel(
    inverse_ref, send_ref, cross_w, cross_b_ref, comp_w_ref, comp_b_ref, other_ref, expert_w_hbm, expert_b_ref, gate_ref,
    out_ref,
    recv, stage, placed, first, expert_w, partial, squeezed, hidden_out, hidden_in,
    load_sem, own_sem, send_sem, recv_sem, comp_send, comp_recv, hid_send, hid_recv,
):
    inner, towers = lax.axis_size("inner"), lax.axis_size("tower")
    me, tower = lax.axis_index("inner"), lax.axis_index("tower")
    _, share, rows = recv.shape
    experts, expert_width, _ = expert_w.shape
    other_width = other_ref.shape[1]
    half = hidden_in.shape[3]
    slots = inverse_ref.shape[0]
    width = stage.shape[1]
    tasks = gate_ref.shape[0] // (experts * towers)

    load_experts = pltpu.make_async_copy(expert_w_hbm, expert_w, load_sem)
    load_experts.start()
    barrier = pltpu.get_barrier_semaphore()
    for off in range(1, inner):
        pl.semaphore_signal(barrier, inc=1, device_id={"inner": lax.rem(me + off, inner)}, device_id_type=MESH)
    for off in range(1, towers):
        pl.semaphore_signal(barrier, inc=1, device_id={"tower": lax.rem(tower + off, towers)}, device_id_type=MESH)
    pl.semaphore_wait(barrier, inner + towers - 2)

    blocks = []
    for off in range(1, inner):
        peer = lax.rem(me + off, inner)
        copy = pltpu.make_async_remote_copy(
            src_ref=send_ref.at[peer],
            dst_ref=recv.at[me],
            send_sem=send_sem.at[off],
            recv_sem=recv_sem.at[off],
            device_id={"inner": peer},
            device_id_type=MESH,
        )
        copy.start()
        blocks.append(copy)
    own = pltpu.make_async_copy(send_ref.at[me], recv.at[me], own_sem)
    own.start()

    other = other_ref[...]
    nt = (((1,), (1,)), ((), ()))
    logits = lax.dot_general(other, gate_ref[:, :other_width], nt, preferred_element_type=jnp.float32)
    load_experts.wait()
    for e in range(experts):
        partial[e] = (
            jnp.dot(other, expert_w[e, :other_width, :], preferred_element_type=jnp.float32) + expert_b_ref[e : e + 1, :]
        )
    own.wait()
    for copy in blocks:
        copy.wait()

    for i in range(inner):
        held = share // width
        stage[i * held : (i + 1) * held] = recv[i].astype(jnp.float32).reshape(held, width, rows)
    for g in range(slots):
        placed[g * width : (g + 1) * width, :] = stage[inverse_ref[g]]
    total = slots * width
    for c in range(0, total, 128):
        first[:, c : c + 128] = placed[c : c + 128, :].T
    base_low = first[...].astype(jnp.bfloat16)
    second = []
    step = 512 if total % 512 == 0 else 128
    for c in range(0, total, step):
        crossed = jnp.dot(base_low, cross_w[:, c : c + step], preferred_element_type=jnp.float32)
        crossed = crossed + cross_b_ref[:, c : c + step]
        base = first[:, c : c + step]
        second.append((base * crossed + base).astype(jnp.bfloat16))
    second = jnp.concatenate(second, axis=1)
    packed = lax.dot_general(second, comp_w_ref[...], nt, preferred_element_type=jnp.float32) + comp_b_ref[...]
    squeezed[tower] = packed.astype(jnp.bfloat16)
    shares = []
    for off in range(1, towers):
        copy = pltpu.make_async_remote_copy(
            src_ref=squeezed.at[tower],
            dst_ref=squeezed.at[tower],
            send_sem=comp_send.at[off],
            recv_sem=comp_recv.at[off],
            device_id={"tower": lax.rem(tower + off, towers)},
            device_id_type=MESH,
        )
        copy.start()
        shares.append(copy)
    for copy in shares:
        copy.wait()

    tail = jnp.concatenate([squeezed[t] for t in range(towers)], axis=1)
    mixes = []
    for e in range(experts):
        value = partial[e] + jnp.dot(tail, expert_w[e, other_width:, :], preferred_element_type=jnp.float32)
        value = jnp.maximum(value, 0.0).astype(jnp.bfloat16)
        for t in range(towers):
            hidden_out[t, e] = value[:, t * half : (t + 1) * half]
        for off in range(1, towers):
            peer = lax.rem(tower + off, towers)
            copy = pltpu.make_async_remote_copy(
                src_ref=hidden_out.at[peer, e],
                dst_ref=hidden_in.at[tower, e],
                send_sem=hid_send.at[off, e],
                recv_sem=hid_recv.at[off, e],
                device_id={"tower": peer},
                device_id_type=MESH,
            )
            copy.start()
            mixes.append(copy)
        hidden_in[tower, e] = hidden_out[tower, e]
    logits = logits + lax.dot_general(tail, gate_ref[:, other_width:], nt, preferred_element_type=jnp.float32)
    weights = jnp.exp(logits)
    count = experts * towers
    gates = []
    for k in range(tasks):
        mine = weights[:, k * count : (k + 1) * count]
        gates.append(mine / jnp.sum(mine, axis=1, keepdims=True))
    for copy in mixes:
        copy.wait()
    for r in range(0, rows, 32):
        sums = [jnp.zeros((32, half), jnp.float32) for _ in range(tasks)]
        for t in range(towers):
            for e in range(experts):
                value = hidden_in[t, e, r : r + 32, :].astype(jnp.float32)
                m = t * experts + e
                sums = [sums[k] + gates[k][r : r + 32, m : m + 1] * value for k in range(tasks)]
        for k in range(tasks):
            out_ref[r : r + 32, k * half : (k + 1) * half] = sums[k].astype(out_ref.dtype)


def dense(inverse, sendable, cross_w, cross_b, comp_w, comp_b, other, expert_w, expert_b, gate):
    inner, share, rows = sendable.shape
    towers = lax.axis_size("tower")
    total = cross_w.shape[0]
    experts, _, hid = expert_w.shape
    tasks = gate.shape[0] // (experts * towers)
    half = hid // towers
    low, full = jnp.bfloat16, jnp.float32
    vmem = pl.BlockSpec(memory_space=pltpu.VMEM)
    smem = pl.BlockSpec(memory_space=pltpu.SMEM)
    dma = pltpu.SemaphoreType.DMA
    return pl.pallas_call(
        dense_kernel,
        out_shape=jax.ShapeDtypeStruct((rows, tasks * half), low),
        in_specs=[smem] + [vmem] * 6 + [pl.BlockSpec(memory_space=pltpu.HBM)] + [vmem] * 2,
        out_specs=vmem,
        scratch_shapes=[
            pltpu.VMEM((inner, share, rows), low),
            pltpu.VMEM((inverse.shape[0], total // inverse.shape[0], rows), full),
            pltpu.VMEM((total, rows), full),
            pltpu.VMEM((rows, total), full),
            pltpu.VMEM(expert_w.shape, low),
            pltpu.VMEM((experts, rows, hid), full),
            pltpu.VMEM((towers, rows, comp_w.shape[0]), low),
            pltpu.VMEM((towers, experts, rows, half), low),
            pltpu.VMEM((towers, experts, rows, half), low),
            dma,
            dma,
            dma((inner,)),
            dma((inner,)),
            dma((towers,)),
            dma((towers,)),
            dma((towers, experts)),
            dma((towers, experts)),
        ],
        compiler_params=pltpu.CompilerParams(collective_id=0, has_side_effects=True, vmem_limit_bytes=24 * 2**20),
    )(inverse, sendable, cross_w, cross_b, comp_w, comp_b, other, expert_w, expert_b, gate)


def on_device(
    ids, bag_len, slot_of_feature, tables, cross_w, cross_b, comp_w, comp_b, other_towers, expert_w, expert_b, gate_w
):
    sendable = pool(tables[0], ids[0], bag_len[0], lax.axis_size("inner"))
    slots = jnp.arange(slot_of_feature.shape[1], dtype=jnp.int32)
    inverse = jnp.sum(jnp.where(slot_of_feature[0][:, None] == slots[None, :], slots[:, None], 0), axis=0)
    ein, tasks, experts = gate_w.shape
    gate = jnp.transpose(gate_w, (1, 2, 0)).reshape(tasks * experts, ein)
    mixed = dense(
        inverse, sendable, cross_w[0], cross_b, jnp.transpose(comp_w[0]), comp_b, other_towers, expert_w, expert_b, gate
    )
    return mixed.reshape(mixed.shape[0], tasks, -1)


def solution(mesh):
    return jax.shard_map(
        on_device,
        mesh=mesh,
        in_specs=(
            P("tower", "inner", "groups", None),
            P("tower", "inner", "groups"),
            P("tower", None),
            P("tower", "inner", None, None),
            P("tower", None, None),
            P("tower", None),
            P("tower", None, None),
            P("tower", None),
            P(("groups", "inner"), None),
            P("tower", None, None),
            P("tower", None),
            P(),
        ),
        out_specs=P(("groups", "inner"), None, "tower"),
        check_vma=False,
    )
```

```python
import functools
import jax
import jax.numpy as jnp
from jax import lax
from jax.experimental import pallas as pl
from jax.experimental.pallas import tpu as pltpu
from jax.sharding import PartitionSpec as P

MESH = pl.DeviceIdType.MESH


def pool_kernel(bag, ids_ref, tab_hbm, out_ref, tab_ref, rows_a, rows_b, acc_ref, sem):
    features, width, vocab = tab_ref.shape
    dests, _, block = out_ref.shape
    samples = dests * block
    lanes = acc_ref.shape[1]
    group = max(g for g in range(1, features + 1) if features % g == 0 and g * width <= lanes)
    steps = vocab // lanes
    each = samples // steps
    rows = (rows_a, rows_b)
    lane = lax.broadcasted_iota(jnp.int32, (1, lanes), 1)
    inside = [lane < (f + 1) * width for f in range(group)]
    loads = []
    for i in range(features // group):
        part = pl.ds(i * group, group)
        loads.append(pltpu.make_async_copy(tab_hbm.at[part], tab_ref.at[part], sem.at[i]))
        loads[-1].start()

    def turn(i, c):
        at = pl.multiple_of(c * lanes, lanes)
        parts = [tab_ref[i * group + f, :, pl.ds(at, lanes)].astype(jnp.float32) for f in range(group)]
        if lanes > group * width:
            parts.append(jnp.zeros((lanes - group * width, lanes), jnp.float32))
        rows[i % 2][pl.ds(at, lanes), :] = jnp.concatenate(parts, axis=0).T

    def look(i, c):
        base = c * each
        held = rows[i % 2]
        for u in range(each):
            total = None
            for f in reversed(range(group)):
                got = []
                for j in range(bag):
                    at = ((i * group + f) * bag + j) * samples + u
                    got.append(held[pl.ds(ids_ref.at[pl.ds(at, samples)][base], 1), :])
                while len(got) > 1:
                    got = [a + b for a, b in zip(got[::2], got[1::2])] + got[len(got) & ~1 :]
                total = got[0] if total is None else jnp.where(inside[f], got[0], total)
            acc_ref[pl.ds(base + u, 1), :] = total

    for held in rows:
        held[pl.ds(vocab, 8), :] = jnp.zeros((8, lanes), jnp.float32)
    count = features // group
    for phase in range(count + 1):
        if phase < count:
            loads[phase].wait()

        def body(c, carry):
            if phase < count:
                turn(phase, c)
            if phase > 0:
                look(phase - 1, c)
            return carry

        lax.fori_loop(0, steps, body, 0)
        if phase > 0:
            first = (phase - 1) * group * width
            for d in range(dests):
                turned = acc_ref[pl.ds(d * block, block), :].T
                out_ref[d, first : first + group * width, :] = turned[: group * width].astype(out_ref.dtype)


def pool(tables, ids, lengths, dests):
    features, vocab, width = tables.shape
    samples, bag = ids.shape[1:]
    in_bag = jnp.arange(bag)[None, :, None] < lengths[:, None, :]
    flat = jnp.where(in_bag, jnp.transpose(ids, (0, 2, 1)), vocab).reshape(-1)
    flat = jnp.pad(flat, (0, 1024))
    return pl.pallas_call(
        functools.partial(pool_kernel, bag),
        out_shape=jax.ShapeDtypeStruct((dests, features * width, samples // dests), jnp.bfloat16),
        in_specs=[pl.BlockSpec(memory_space=pltpu.SMEM), pl.BlockSpec(memory_space=pltpu.HBM)],
        out_specs=pl.BlockSpec(memory_space=pltpu.VMEM),
        scratch_shapes=[
            pltpu.VMEM((features, width, vocab), jnp.bfloat16),
            pltpu.VMEM((vocab + 8, 128), jnp.float32),
            pltpu.VMEM((vocab + 8, 128), jnp.float32),
            pltpu.VMEM((samples, 128), jnp.float32),
            pltpu.SemaphoreType.DMA((features,)),
        ],
        compiler_params=pltpu.CompilerParams(vmem_limit_bytes=48 * 2**20),
    )(flat, jnp.transpose(tables, (0, 2, 1)))


def dense_kernel(
    inverse_ref, send_ref, cross_w, cross_b_ref, comp_w_ref, comp_b_ref, other_ref, expert_w_hbm, expert_b_ref, gate_ref,
    out_ref,
    recv, stage, placed, first, expert_w, partial, squeezed, hidden_out, hidden_in,
    load_sem, own_sem, send_sem, recv_sem, comp_send, comp_recv, hid_send, hid_recv,
):
    inner, towers = lax.axis_size("inner"), lax.axis_size("tower")
    me, tower = lax.axis_index("inner"), lax.axis_index("tower")
    _, share, rows = recv.shape
    experts, expert_width, _ = expert_w.shape
    other_width = other_ref.shape[1]
    half = hidden_in.shape[3]
    slots = inverse_ref.shape[0]
    width = stage.shape[1]
    tasks = gate_ref.shape[0] // (experts * towers)

    load_experts = pltpu.make_async_copy(expert_w_hbm, expert_w, load_sem)
    load_experts.start()
    barrier = pltpu.get_barrier_semaphore()
    for off in range(1, inner):
        pl.semaphore_signal(barrier, inc=1, device_id={"inner": lax.rem(me + off, inner)}, device_id_type=MESH)
    for off in range(1, towers):
        pl.semaphore_signal(barrier, inc=1, device_id={"tower": lax.rem(tower + off, towers)}, device_id_type=MESH)
    pl.semaphore_wait(barrier, inner + towers - 2)

    blocks = []
    for off in range(1, inner):
        peer = lax.rem(me + off, inner)
        copy = pltpu.make_async_remote_copy(
            src_ref=send_ref.at[peer],
            dst_ref=recv.at[me],
            send_sem=send_sem.at[off],
            recv_sem=recv_sem.at[off],
            device_id={"inner": peer},
            device_id_type=MESH,
        )
        copy.start()
        blocks.append(copy)
    own = pltpu.make_async_copy(send_ref.at[me], recv.at[me], own_sem)
    own.start()

    other = other_ref[...]
    nt = (((1,), (1,)), ((), ()))
    logits = lax.dot_general(other, gate_ref[:, :other_width], nt, preferred_element_type=jnp.float32)
    load_experts.wait()
    for e in range(experts):
        partial[e] = (
            jnp.dot(other, expert_w[e, :other_width, :], preferred_element_type=jnp.float32) + expert_b_ref[e : e + 1, :]
        )
    own.wait()
    for copy in blocks:
        copy.wait()

    for i in range(inner):
        held = share // width
        stage[i * held : (i + 1) * held] = recv[i].astype(jnp.float32).reshape(held, width, rows)
    for g in range(slots):
        placed[g * width : (g + 1) * width, :] = stage[inverse_ref[g]]
    total = slots * width
    for c in range(0, total, 128):
        first[:, c : c + 128] = placed[c : c + 128, :].T
    base_low = first[...].astype(jnp.bfloat16)
    second = []
    step = 512 if total % 512 == 0 else 128
    for c in range(0, total, step):
        crossed = jnp.dot(base_low, cross_w[:, c : c + step], preferred_element_type=jnp.float32)
        crossed = crossed + cross_b_ref[:, c : c + step]
        base = first[:, c : c + step]
        second.append((base * crossed + base).astype(jnp.bfloat16))
    second = jnp.concatenate(second, axis=1)
    packed = lax.dot_general(second, comp_w_ref[...], nt, preferred_element_type=jnp.float32) + comp_b_ref[...]
    squeezed[tower] = packed.astype(jnp.bfloat16)
    shares = []
    for off in range(1, towers):
        copy = pltpu.make_async_remote_copy(
            src_ref=squeezed.at[tower],
            dst_ref=squeezed.at[tower],
            send_sem=comp_send.at[off],
            recv_sem=comp_recv.at[off],
            device_id={"tower": lax.rem(tower + off, towers)},
            device_id_type=MESH,
        )
        copy.start()
        shares.append(copy)
    for copy in shares:
        copy.wait()

    tail = jnp.concatenate([squeezed[t] for t in range(towers)], axis=1)
    mixes = []
    for e in range(experts):
        value = partial[e] + jnp.dot(tail, expert_w[e, other_width:, :], preferred_element_type=jnp.float32)
        value = jnp.maximum(value, 0.0).astype(jnp.bfloat16)
        for t in range(towers):
            hidden_out[t, e] = value[:, t * half : (t + 1) * half]
        for off in range(1, towers):
            peer = lax.rem(tower + off, towers)
            copy = pltpu.make_async_remote_copy(
                src_ref=hidden_out.at[peer, e],
                dst_ref=hidden_in.at[tower, e],
                send_sem=hid_send.at[off, e],
                recv_sem=hid_recv.at[off, e],
                device_id={"tower": peer},
                device_id_type=MESH,
            )
            copy.start()
            mixes.append(copy)
        hidden_in[tower, e] = hidden_out[tower, e]
    logits = logits + lax.dot_general(tail, gate_ref[:, other_width:], nt, preferred_element_type=jnp.float32)
    weights = jnp.exp(logits)
    count = experts * towers
    gates = []
    for k in range(tasks):
        mine = weights[:, k * count : (k + 1) * count]
        gates.append(mine / jnp.sum(mine, axis=1, keepdims=True))
    for copy in mixes:
        copy.wait()
    for r in range(0, rows, 32):
        sums = [jnp.zeros((32, half), jnp.float32) for _ in range(tasks)]
        for t in range(towers):
            for e in range(experts):
                value = hidden_in[t, e, r : r + 32, :].astype(jnp.float32)
                m = t * experts + e
                sums = [sums[k] + gates[k][r : r + 32, m : m + 1] * value for k in range(tasks)]
        for k in range(tasks):
            out_ref[r : r + 32, k * half : (k + 1) * half] = sums[k].astype(out_ref.dtype)


def dense(inverse, sendable, cross_w, cross_b, comp_w, comp_b, other, expert_w, expert_b, gate):
    inner, share, rows = sendable.shape
    towers = lax.axis_size("tower")
    total = cross_w.shape[0]
    experts, _, hid = expert_w.shape
    tasks = gate.shape[0] // (experts * towers)
    half = hid // towers
    low, full = jnp.bfloat16, jnp.float32
    vmem = pl.BlockSpec(memory_space=pltpu.VMEM)
    smem = pl.BlockSpec(memory_space=pltpu.SMEM)
    dma = pltpu.SemaphoreType.DMA
    return pl.pallas_call(
        dense_kernel,
        out_shape=jax.ShapeDtypeStruct((rows, tasks * half), low),
        in_specs=[smem] + [vmem] * 6 + [pl.BlockSpec(memory_space=pltpu.HBM)] + [vmem] * 2,
        out_specs=vmem,
        scratch_shapes=[
            pltpu.VMEM((inner, share, rows), low),
            pltpu.VMEM((inverse.shape[0], total // inverse.shape[0], rows), full),
            pltpu.VMEM((total, rows), full),
            pltpu.VMEM((rows, total), full),
            pltpu.VMEM(expert_w.shape, low),
            pltpu.VMEM((experts, rows, hid), full),
            pltpu.VMEM((towers, rows, comp_w.shape[0]), low),
            pltpu.VMEM((towers, experts, rows, half), low),
            pltpu.VMEM((towers, experts, rows, half), low),
            dma,
            dma,
            dma((inner,)),
            dma((inner,)),
            dma((towers,)),
            dma((towers,)),
            dma((towers, experts)),
            dma((towers, experts)),
        ],
        compiler_params=pltpu.CompilerParams(collective_id=0, has_side_effects=True, vmem_limit_bytes=24 * 2**20),
    )(inverse, sendable, cross_w, cross_b, comp_w, comp_b, other, expert_w, expert_b, gate)


def on_device(
    ids, bag_len, slot_of_feature, tables, cross_w, cross_b, comp_w, comp_b, other_towers, expert_w, expert_b, gate_w
):
    sendable = pool(tables[0], ids[0], bag_len[0], lax.axis_size("inner"))
    slots = jnp.arange(slot_of_feature.shape[1], dtype=jnp.int32)
    inverse = jnp.sum(jnp.where(slot_of_feature[0][:, None] == slots[None, :], slots[:, None], 0), axis=0)
    ein, tasks, experts = gate_w.shape
    gate = jnp.transpose(gate_w, (1, 2, 0)).reshape(tasks * experts, ein)
    mixed = dense(
        inverse, sendable, cross_w[0], cross_b, jnp.transpose(comp_w[0]), comp_b, other_towers, expert_w, expert_b, gate
    )
    return mixed.reshape(mixed.shape[0], tasks, -1)


def solution(mesh):
    return jax.shard_map(
        on_device,
        mesh=mesh,
        in_specs=(
            P("tower", "inner", "groups", None),
            P("tower", "inner", "groups"),
            P("tower", None),
            P("tower", "inner", None, None),
            P("tower", None, None),
            P("tower", None),
            P("tower", None, None),
            P("tower", None),
            P(("groups", "inner"), None),
            P("tower", None, None),
            P("tower", None),
            P(),
        ),
        out_specs=P(("groups", "inner"), None, "tower"),
        check_vma=False,
    )
```
